32 devices in a mesh: fsdp: 16 (over z, y, core), frame: 2 (over x).
Axes of the slice: x: 2, y: 2, z: 4, core: 2. Of those that a mesh axis runs over, the one named last changes fastest.
Arguments:
- student_tokens: bfloat16 [16, 8, 256, 3200], P('fsdp', 'frame'), may hold values from -6 to 6
- norm_gain: float32 [3200], replicated, may hold values from 0.1 to 1.9
- mae_weight: bfloat16 [3200, 1408], P('fsdp'), may hold values from -0.109375 to 0.109375
- clip_target: bfloat16 [16, 8, 3200], P('fsdp', 'frame'), may hold values from -6 to 6
- mae_target: bfloat16 [16, 8, 128, 1408], P('fsdp', 'frame'), may hold values from -6 to 6
- keep_mask: int32 [16, 8, 256], P('fsdp', 'frame'), may hold values 0 or 1
- teacher_gate: int32 [16], P('fsdp'), may hold values from 0 to 2
- temp_bucket: int32 [16], P('fsdp'), may hold values from 0 to 3
Outputs:
- token_grad: bfloat16 [16, 8, 256, 3200], P('fsdp', 'frame')
- weight_grad: float32 [3200, 1408], P('fsdp')
- gain_grad: float32 [3200], replicated
- loss: float32 [], replicated
The draws below stay inside these ranges and needn't reach their ends.
Inputs may be any that keep to these rules, and one draw needn't show every extreme that they name: `teacher_gate`: 0 aligns a clip to both teachers, 1 to InternVL only, 2 to VideoMAE-g only.
All inputs are finite; a program needn't handle non-finite values. No bound on the sum of `keep_mask` on one device may be relied on, other than what follows from the above.
Results may differ from the reference program's by a relative error of at most 0.011.
Values may be sent and summed in bfloat16 or wider, within the bound.
A program may use at most 128 MiB of HBM per device.

```python
import jax
import jax.numpy as jnp
from jax import lax

D = 3200
TEACHER_WIDTH = 1408
FRAMES = 8
PATCHES = 256
HALF = 128
BATCH = 16


def set_ends(entries, stream_key, least, largest):
    place = [jax.random.randint(jax.random.fold_in(stream_key, axis), (), 0, length) for axis, length in enumerate(entries.shape)]
    longest = entries.shape.index(max(entries.shape))
    next_to = place[:longest] + [(place[longest] + 1) % entries.shape[longest]] + place[longest + 1:]
    return entries.at[tuple(place)].set(least).at[tuple(next_to)].set(largest)


def steps_of(rng, shape, pieces, smallest, top_value):
    def one(position, blocks):
        heights = jax.random.uniform(jax.random.fold_in(jax.random.fold_in(rng, 6), position), (blocks,), jnp.float32, smallest / len(pieces), top_value / len(pieces))
        return jnp.repeat(jnp.exp(heights), shape[position] // blocks).reshape((-1,) + (1,) * (len(shape) - position - 1))

    loudness = one(*pieces[0])
    for cut in pieces[1:]:
        loudness = loudness * one(*cut)
    return loudness


def bell_draw(stream_key, dims, scale, limit, cuts=(), dtype=jnp.bfloat16):
    values = jax.random.normal(stream_key, dims, jnp.float32) * scale
    if len(cuts) > 0:
        values = steps_of(stream_key, dims, cuts, -0.22, 0.18) * values
    return jnp.clip(values, min=-limit, max=limit).astype(dtype)


def setup_inputs(seed: int = 0) -> dict:
    seeds = jax.random.split(jax.random.key(seed), 9)
    student_tokens = bell_draw(seeds[0], (BATCH, FRAMES, PATCHES, D), 1.0, 6.0, ((0, 16), (1, 2)))
    norm_gain = jnp.clip(1.0 + 0.18 * jax.random.normal(seeds[1], (D,), jnp.float32), 0.1, 1.9)
    mae_weight = bell_draw(seeds[2], (D, TEACHER_WIDTH), D ** -0.5, 0.109375, ((0, 16),))
    clip_target = bell_draw(seeds[3], (BATCH, FRAMES, D), 1.0, 6.0, ((0, 16), (1, 2)))
    mae_target = bell_draw(seeds[4], (BATCH, FRAMES, HALF, TEACHER_WIDTH), 1.0, 6.0, ((0, 16), (1, 2)))
    keep_mask = set_ends((jax.random.randint(seeds[5], (BATCH, FRAMES, PATCHES), 0, 2) < 1).astype(jnp.int32), jax.random.fold_in(seeds[5], 1), 0, 1)
    teacher_gate = set_ends(jax.random.randint(seeds[6], (BATCH,), 0, 3), jax.random.fold_in(seeds[6], 1), 0, 2).astype(jnp.int32)
    temp_bucket = set_ends(jax.random.randint(seeds[7], (BATCH,), 0, 4), jax.random.fold_in(seeds[7], 1), 0, 3).astype(jnp.int32)
    return {"student_tokens": student_tokens, "norm_gain": norm_gain, "mae_weight": mae_weight, "clip_target": clip_target, "mae_target": mae_target, "keep_mask": keep_mask, "teacher_gate": teacher_gate, "temp_bucket": temp_bucket}


epsilon = 1e-06

def unit_rows(values):
    inverse = lax.rsqrt(lax.optimization_barrier(jnp.mean(values * values, axis=-1, keepdims=True)) + epsilon)
    return (values * inverse, inverse)

def unit_grad(errors, unit, inverse):
    return inverse * (errors - unit * lax.optimization_barrier(jnp.mean(errors * unit, axis=-1, keepdims=True)))

def reference(student_tokens, norm_gain, mae_weight, clip_target, mae_target, keep_mask, teacher_gate, temp_bucket):
    middle = FRAMES // 2

    def one_sample(carry, inputs):
        weight_sum, gain_sum, loss_sum = carry
        tokens, keeping, clip_rows, mae_rows, gate_value, bucket_value = inputs
        token_float = tokens.astype(jnp.float32)
        recip = lax.rsqrt(lax.optimization_barrier(jnp.mean(token_float * token_float, axis=-1, keepdims=True)) + epsilon)
        normed = (token_float * recip * norm_gain).astype(jnp.bfloat16)
        keep_float = keeping.astype(jnp.float32)
        pooled = jnp.einsum('fp,fpd->fd', keep_float, normed.astype(jnp.float32), precision=lax.Precision.HIGHEST) / PATCHES
        clip_unit, clip_inverse = unit_rows(pooled)
        teach_unit, unused_one = unit_rows(clip_rows.astype(jnp.float32))
        clip_err = clip_unit - teach_unit
        clip_loss = 0.5 * lax.optimization_barrier(jnp.sum(clip_err * clip_err, axis=-1))
        scaling = jnp.exp2(bucket_value.astype(jnp.float32))
        clip_on = (gate_value != 2).astype(jnp.float32)
        mae_on = (gate_value != 1).astype(jnp.float32)
        pairs = normed.reshape(2, middle, 2, HALF, D)
        first_rows = jnp.transpose(pairs[0], (1, 0, 2, 3)).reshape(-1, D)
        second_rows = jnp.transpose(pairs[1], (1, 0, 2, 3)).reshape(-1, D)
        keep_pairs = keep_float.reshape(2, middle, 2, HALF)
        live = jnp.transpose(keep_pairs[0] * keep_pairs[1], (1, 0, 2)).reshape(-1)
        projected = 0.5 * (jnp.dot(first_rows, mae_weight, preferred_element_type=jnp.float32) + jnp.dot(second_rows, mae_weight, preferred_element_type=jnp.float32))
        proj_unit, proj_inverse = unit_rows(projected)
        target_unit, unused_two = unit_rows(mae_rows.reshape(-1, TEACHER_WIDTH).astype(jnp.float32))
        mae_err = proj_unit - target_unit
        mae_loss = 0.5 * lax.optimization_barrier(jnp.sum(mae_err * mae_err, axis=-1))
        sample_loss = scaling * (clip_on * jnp.sum(clip_loss) + mae_on * jnp.sum(live * mae_loss))
        row_grad = ((scaling * mae_on * live)[:, None] * unit_grad(mae_err, proj_unit, proj_inverse)).astype(jnp.bfloat16)
        pair_grad = (0.5 * jnp.dot(row_grad, mae_weight.T, preferred_element_type=jnp.float32)).astype(jnp.bfloat16)
        weight_part = 0.5 * (jnp.dot(first_rows.T, row_grad, preferred_element_type=jnp.float32) + jnp.dot(second_rows.T, row_grad, preferred_element_type=jnp.float32))
        clip_grad = scaling * clip_on * unit_grad(clip_err, clip_unit, clip_inverse)
        arranged = jnp.transpose(pair_grad.reshape(2, middle, HALF, D), (1, 0, 2, 3)).reshape(1, middle, PATCHES, D)
        spread = jnp.broadcast_to(arranged, (2, middle, PATCHES, D)).reshape(FRAMES, PATCHES, D).astype(jnp.float32)
        normed_grad = spread + keep_float[:, :, None] * clip_grad[:, None, :] / PATCHES
        inner = lax.optimization_barrier(jnp.mean(normed_grad * norm_gain * token_float, axis=-1, keepdims=True))
        token_grad = (recip * (norm_gain * normed_grad - token_float * recip * recip * inner)).astype(jnp.bfloat16)
        gain_part = lax.optimization_barrier(jnp.sum(normed_grad * token_float * recip, axis=(0, 1)))
        return ((weight_sum + weight_part, gain_sum + gain_part, loss_sum + sample_loss), token_grad)
    start = (jnp.zeros((D, TEACHER_WIDTH), jnp.float32), jnp.zeros((D,), jnp.float32), jnp.zeros((), jnp.float32))
    totals, token_grad = lax.scan(one_sample, start, (student_tokens, keep_mask, clip_target, mae_target, teacher_gate, temp_bucket))
    weight_sum, gain_sum, loss_sum = totals
    weight_grad = weight_sum / BATCH
    gain_grad = gain_sum / BATCH
    loss = loss_sum / (BATCH * FRAMES * PATCHES * TEACHER_WIDTH)
    return (token_grad, weight_grad, gain_grad, loss)
```

```python
import jax
import jax.numpy as jnp
from jax import lax
from jax.sharding import PartitionSpec as P

epsilon = 1e-06


def swapped(shard, axis, stride):
    return lax.ppermute(shard, axis, [(i, i ^ 1 << stride) for i in range(lax.axis_size(axis))])


def unit_rows(values):
    inverse = lax.rsqrt(jnp.mean(values * values, axis=-1, keepdims=True) + epsilon)
    return (values * inverse, inverse)


def unit_grad(errors, unit, inverse):
    return inverse * (errors - unit * jnp.mean(errors * unit, axis=-1, keepdims=True))


def over_rows(left, right):
    return lax.dot_general(
        left, right, (((0,), (0,)), ((), ())), preferred_element_type=jnp.float32
    ).astype(jnp.bfloat16)


def doubled_sum(values, axes):
    for axis in axes:
        for stride in range(lax.axis_size(axis).bit_length() - 1):
            values = values + swapped(values, axis, stride)
    return values


def back_project(grads, weight):
    return (
        0.5
        * lax.dot_general(
            grads, weight, (((1,), (1,)), ((), ())), preferred_element_type=jnp.float32
        )
    ).astype(jnp.bfloat16)


def per_device(
    student_tokens,
    norm_gain,
    mae_weight,
    clip_target,
    mae_target,
    keep_mask,
    teacher_gate,
    temp_bucket,
):
    samples, frames_here, patches, model_width = student_tokens.shape
    half_rows = patches // 2
    channels = mae_weight.shape[1]
    frame_devices = lax.axis_size("frame")
    top_bit = frame_devices.bit_length() - 2
    weight = lax.all_gather(mae_weight, "fsdp", axis=0, tiled=True)
    token_float = student_tokens.astype(jnp.float32)
    recip = lax.rsqrt(jnp.mean(token_float * token_float, axis=-1, keepdims=True) + epsilon)
    normed = (token_float * recip * norm_gain).astype(jnp.bfloat16)
    keep_float = keep_mask.astype(jnp.float32)
    pooled = (
        jnp.einsum(
            "bfp,bfpd->bfd",
            keep_mask.astype(jnp.bfloat16),
            normed,
            preferred_element_type=jnp.float32,
        )
        / patches
    )
    clip_unit, clip_inverse = unit_rows(pooled)
    teach_unit, unused_one = unit_rows(clip_target.astype(jnp.float32))
    clip_err = clip_unit - teach_unit
    clip_loss = 0.5 * jnp.sum(clip_err * clip_err, axis=-1)
    scaling = jnp.exp2(temp_bucket.astype(jnp.float32))
    clip_on = (teacher_gate != 2).astype(jnp.float32)
    mae_on = (teacher_gate != 1).astype(jnp.float32)
    parity = lax.axis_index("frame") // (frame_devices // 2)
    halves = normed.reshape(samples, frames_here, 2, half_rows, model_width)
    mask_halves = keep_mask.astype(jnp.bfloat16).reshape(samples, frames_here, 2, half_rows)
    own_half = lax.dynamic_slice_in_dim(halves, parity, 1, 2)[:, :, 0]
    sent_half = lax.dynamic_slice_in_dim(halves, 1 - parity, 1, 2)[:, :, 0]
    own_mask = lax.dynamic_slice_in_dim(mask_halves, parity, 1, 2)[:, :, 0]
    sent_mask = lax.dynamic_slice_in_dim(mask_halves, 1 - parity, 1, 2)[:, :, 0]
    got_half, got_mask = swapped((sent_half, sent_mask), "frame", top_bit)
    mean_rows = (
        (0.5 * (own_half.astype(jnp.float32) + got_half.astype(jnp.float32)))
        .astype(jnp.bfloat16)
        .reshape(-1, model_width)
    )
    live = (own_mask.astype(jnp.float32) * got_mask.astype(jnp.float32)).reshape(samples, -1)
    projected = jnp.dot(mean_rows, weight, preferred_element_type=jnp.float32)
    proj_unit, proj_inverse = unit_rows(projected)
    target_unit, unused_two = unit_rows(mae_target.reshape(-1, channels).astype(jnp.float32))
    mae_err = proj_unit - target_unit
    mae_loss = (0.5 * jnp.sum(mae_err * mae_err, axis=-1)).reshape(samples, -1)
    sample_loss = scaling * (
        clip_on * jnp.sum(clip_loss, axis=1) + mae_on * jnp.sum(live * mae_loss, axis=1)
    )
    row_scale = ((scaling * mae_on)[:, None] * live).reshape(-1)
    row_grad = (row_scale[:, None] * unit_grad(mae_err, proj_unit, proj_inverse)).astype(
        jnp.bfloat16
    )
    returned = swapped(row_grad, "frame", top_bit)
    clip_count = samples * lax.axis_size("fsdp")
    cut = channels // 256 // 2 * 256 + 128
    shards = []
    for start, stop in ((0, cut), (cut, channels)):
        shard = lax.psum_scatter(
            over_rows(mean_rows, row_grad[:, start:stop]),
            "fsdp",
            scatter_dimension=0,
            tiled=True,
        )
        shards.append(shard)
    own_grads = row_grad.reshape(samples, frames_here, half_rows, channels)
    got_grads = returned.reshape(samples, frames_here, half_rows, channels)
    lower = jnp.where(parity == 0, own_grads, got_grads)
    upper = jnp.where(parity == 0, got_grads, own_grads)
    both_grads = jnp.stack([lower, upper], axis=2).reshape(-1, channels)
    spread = (
        back_project(both_grads, weight)
        .reshape(samples, frames_here, patches, model_width)
        .astype(jnp.float32)
    )
    clip_grad = (scaling * clip_on)[:, None, None] * unit_grad(clip_err, clip_unit, clip_inverse)
    normed_grad = spread + keep_float[:, :, :, None] * clip_grad[:, :, None, :] / patches
    inner = jnp.mean(normed_grad * norm_gain * token_float, axis=-1, keepdims=True)
    token_grad = (recip * (norm_gain * normed_grad - token_float * recip * recip * inner)).astype(
        jnp.bfloat16
    )
    gain_local = jnp.sum(normed_grad * token_float * recip, axis=(0, 1, 2))
    loss_local = jnp.sum(sample_loss)
    sums = jnp.concatenate([gain_local, jnp.full((128,), loss_local)])
    sums = doubled_sum(sums, ("fsdp", "frame"))
    gain_total, loss_total = sums[:model_width], sums[model_width]
    frame_strides = range(frame_devices.bit_length() - 1)
    whole = []
    for shard in shards:
        total = shard.astype(jnp.float32)
        for stride in frame_strides:
            total = lax.reduce_precision(total, 8, 7)
            sent = total.astype(jnp.bfloat16)
            total = total + swapped(sent, "frame", stride).astype(jnp.float32)
        whole.append(total)
    weight_grad = jnp.concatenate(whole, axis=1) / clip_count
    frame_count = frames_here * frame_devices
    gain_grad = gain_total / clip_count
    loss = loss_total / (clip_count * frame_count * patches * channels)
    return (token_grad, weight_grad, gain_grad, loss)


def solution(mesh):
    placed = (
        P("fsdp", "frame", None, None),
        P(),
        P("fsdp", None),
        P("fsdp", "frame", None),
        P("fsdp", "frame", None, None),
        P("fsdp", "frame", None),
        P("fsdp"),
        P("fsdp"),
    )
    return jax.shard_map(
        per_device,
        mesh=mesh,
        in_specs=placed,
        out_specs=(P("fsdp", "frame", None, None), P("fsdp", None), P(), P()),
        check_vma=False,
    )
```

```python
import jax
import jax.numpy as jnp
from jax import lax
from jax.sharding import PartitionSpec as P

epsilon = 1e-06


def swapped(shard, axis, stride):
    return lax.ppermute(shard, axis, [(i, i ^ 1 << stride) for i in range(lax.axis_size(axis))])


def unit_rows(values):
    inverse = lax.rsqrt(jnp.mean(values * values, axis=-1, keepdims=True) + epsilon)
    return (values * inverse, inverse)


def unit_grad(errors, unit, inverse):
    return inverse * (errors - unit * jnp.mean(errors * unit, axis=-1, keepdims=True))


def over_rows(left, right):
    return lax.dot_general(
        left, right, (((0,), (0,)), ((), ())), preferred_element_type=jnp.float32
    ).astype(jnp.bfloat16)


def doubled_sum(values, axes):
    for axis in axes:
        for stride in range(lax.axis_size(axis).bit_length() - 1):
            values = values + swapped(values, axis, stride)
    return values


def halved(partial, axis, stride):
    bit = lax.axis_index(axis) >> stride & 1
    pairs = partial.reshape(-1, 2, *partial.shape[1:])
    sent = lax.dynamic_index_in_dim(pairs, 1 - bit, 1, keepdims=False)
    kept = lax.dynamic_index_in_dim(pairs, bit, 1, keepdims=False)
    got = swapped(sent, axis, stride)
    return (kept.astype(jnp.float32) + got.astype(jnp.float32)).astype(jnp.bfloat16)


def channel_cuts(channels, pieces):
    tiles = channels // 128
    ends = [-(-tiles * step // pieces) * 128 for step in range(1, pieces)]
    return list(zip([0] + ends, ends + [channels]))


def back_project(grads, weight):
    return (
        0.5
        * lax.dot_general(
            grads, weight, (((1,), (1,)), ((), ())), preferred_element_type=jnp.float32
        )
    ).astype(jnp.bfloat16)


def per_device(
    student_tokens,
    norm_gain,
    mae_weight,
    clip_target,
    mae_target,
    keep_mask,
    teacher_gate,
    temp_bucket,
):
    samples, frames_here, patches, model_width = student_tokens.shape
    half_rows = patches // 2
    channels = mae_weight.shape[1]
    frame_devices = lax.axis_size("frame")
    top_bit = frame_devices.bit_length() - 2
    weight = lax.all_gather(mae_weight, "fsdp", axis=0, tiled=True)
    token_float = student_tokens.astype(jnp.float32)
    recip = lax.rsqrt(jnp.mean(token_float * token_float, axis=-1, keepdims=True) + epsilon)
    normed = (token_float * recip * norm_gain).astype(jnp.bfloat16)
    keep_float = keep_mask.astype(jnp.float32)
    pooled = (
        jnp.einsum(
            "bfp,bfpd->bfd",
            keep_mask.astype(jnp.bfloat16),
            normed,
            preferred_element_type=jnp.float32,
        )
        / patches
    )
    clip_unit, clip_inverse = unit_rows(pooled)
    teach_unit, unused_one = unit_rows(clip_target.astype(jnp.float32))
    clip_err = clip_unit - teach_unit
    clip_loss = 0.5 * jnp.sum(clip_err * clip_err, axis=-1)
    scaling = jnp.exp2(temp_bucket.astype(jnp.float32))
    clip_on = (teacher_gate != 2).astype(jnp.float32)
    mae_on = (teacher_gate != 1).astype(jnp.float32)
    parity = lax.axis_index("frame") // (frame_devices // 2)
    halves = normed.reshape(samples, frames_here, 2, half_rows, model_width)
    mask_halves = keep_mask.astype(jnp.bfloat16).reshape(samples, frames_here, 2, half_rows)
    own_half = lax.dynamic_slice_in_dim(halves, parity, 1, 2)[:, :, 0]
    sent_half = lax.dynamic_slice_in_dim(halves, 1 - parity, 1, 2)[:, :, 0]
    own_mask = lax.dynamic_slice_in_dim(mask_halves, parity, 1, 2)[:, :, 0]
    sent_mask = lax.dynamic_slice_in_dim(mask_halves, 1 - parity, 1, 2)[:, :, 0]
    got_half, got_mask = swapped((sent_half, sent_mask), "frame", top_bit)
    mean_rows = (
        (0.5 * (own_half.astype(jnp.float32) + got_half.astype(jnp.float32)))
        .astype(jnp.bfloat16)
        .reshape(-1, model_width)
    )
    live = (own_mask.astype(jnp.float32) * got_mask.astype(jnp.float32)).reshape(samples, -1)
    projected = jnp.dot(mean_rows, weight, preferred_element_type=jnp.float32)
    proj_unit, proj_inverse = unit_rows(projected)
    target_unit, unused_two = unit_rows(mae_target.reshape(-1, channels).astype(jnp.float32))
    mae_err = proj_unit - target_unit
    mae_loss = (0.5 * jnp.sum(mae_err * mae_err, axis=-1)).reshape(samples, -1)
    sample_loss = scaling * (
        clip_on * jnp.sum(clip_loss, axis=1) + mae_on * jnp.sum(live * mae_loss, axis=1)
    )
    row_scale = ((scaling * mae_on)[:, None] * live).reshape(-1)
    row_grad = (row_scale[:, None] * unit_grad(mae_err, proj_unit, proj_inverse)).astype(
        jnp.bfloat16
    )
    returned = swapped(row_grad, "frame", top_bit)
    clip_count = samples * lax.axis_size("fsdp")
    members = lax.axis_size("fsdp")
    strides = range(members.bit_length() - 1)
    parts = []
    for start, stop in channel_cuts(channels, 3):
        part = over_rows(mean_rows, row_grad[:, start:stop])
        parts.append(halved(part.reshape(members, -1, stop - start), "fsdp", strides[0]))
    row_grad, parts = lax.optimization_barrier((row_grad, parts))
    parts = [halved(part, "fsdp", strides[1]) for part in parts]
    own_grads = row_grad.reshape(samples, frames_here, half_rows, channels)
    got_grads = returned.reshape(samples, frames_here, half_rows, channels)
    lower = jnp.where(parity == 0, own_grads, got_grads)
    upper = jnp.where(parity == 0, got_grads, own_grads)
    both_grads = jnp.stack([lower, upper], axis=2).reshape(-1, channels)
    spread, parts[0] = lax.optimization_barrier((back_project(both_grads, weight), parts[0]))
    parts[0] = halved(parts[0], "fsdp", strides[2])
    spread = spread.reshape(samples, frames_here, patches, model_width).astype(jnp.float32)
    clip_grad = (scaling * clip_on)[:, None, None] * unit_grad(clip_err, clip_unit, clip_inverse)
    normed_grad = spread + keep_float[:, :, :, None] * clip_grad[:, :, None, :] / patches
    inner = jnp.mean(normed_grad * norm_gain * token_float, axis=-1, keepdims=True)
    inner, parts[:2] = lax.optimization_barrier((inner, parts[:2]))
    token_grad = (recip * (norm_gain * normed_grad - token_float * recip * recip * inner)).astype(
        jnp.bfloat16
    )
    gain_local = jnp.sum(normed_grad * token_float * recip, axis=(0, 1, 2))
    loss_local = jnp.sum(sample_loss)
    shards = []
    for index, part in enumerate(parts):
        for stride in strides[3 if index == 0 else 2 :]:
            part = halved(part, "fsdp", stride)
        shards.append(part[0])
    sums = jnp.concatenate([gain_local, jnp.full((128,), loss_local)])
    sums = doubled_sum(sums, ("fsdp", "frame"))
    gain_total, loss_total = sums[:model_width], sums[model_width]
    frame_strides = range(frame_devices.bit_length() - 1)
    whole = []
    for shard in shards:
        total = shard.astype(jnp.float32)
        for stride in frame_strides:
            total = lax.reduce_precision(total, 8, 7)
            sent = total.astype(jnp.bfloat16)
            total = total + swapped(sent, "frame", stride).astype(jnp.float32)
        whole.append(total)
    weight_grad = jnp.concatenate(whole, axis=1) / clip_count
    frame_count = frames_here * frame_devices
    gain_grad = gain_total / clip_count
    loss = loss_total / (clip_count * frame_count * patches * channels)
    return (token_grad, weight_grad, gain_grad, loss)


def solution(mesh):
    placed = (
        P("fsdp", "frame", None, None),
        P(),
        P("fsdp", None),
        P("fsdp", "frame", None),
        P("fsdp", "frame", None, None),
        P("fsdp", "frame", None),
        P("fsdp"),
        P("fsdp"),
    )
    return jax.shard_map(
        per_device,
        mesh=mesh,
        in_specs=placed,
        out_specs=(P("fsdp", "frame", None, None), P("fsdp", None), P(), P()),
        check_vma=False,
    )
```

```python
import jax
import jax.numpy as jnp
from jax import lax
from jax.sharding import PartitionSpec as P


epsilon = 1e-06


def swapped(shard, axis, stride):
    return lax.ppermute(shard, axis, [(i, i ^ 1 << stride) for i in range(lax.axis_size(axis))])


def unit_rows(values):
    inverse = lax.rsqrt(jnp.mean(values * values, axis=-1, keepdims=True) + epsilon)
    return (values * inverse, inverse)


def unit_grad(errors, unit, inverse):
    return inverse * (errors - unit * jnp.mean(errors * unit, axis=-1, keepdims=True))


def over_rows(left, right):
    return lax.dot_general(
        left, right, (((0,), (0,)), ((), ())), preferred_element_type=jnp.float32
    ).astype(jnp.bfloat16)


def doubled_sum(values, axes):
    for axis in axes:
        for stride in range(lax.axis_size(axis).bit_length() - 1):
            values = values + swapped(values, axis, stride)
    return values


def halved(partial, axis, stride, lower):
    bit = lax.axis_index(axis) >> stride & 1
    pairs = partial.reshape(-1, 2, lower, *partial.shape[1:])
    sent = lax.dynamic_index_in_dim(pairs, 1 - bit, 1, keepdims=False)
    kept = lax.dynamic_index_in_dim(pairs, bit, 1, keepdims=False)
    got = swapped(sent, axis, stride)
    added = (kept.astype(jnp.float32) + got.astype(jnp.float32)).astype(jnp.bfloat16)
    return added.reshape(-1, *partial.shape[1:])


def halving_step(parts, orders, steps):
    result = []
    for part, order in zip(parts, orders):
        for step in range(len(order))[steps]:
            lower = 1 << sum(other < order[step] for other in order[step + 1 :])
            part = halved(part, "fsdp", order[step], lower)
        result.append(part)
    return result


def channel_cuts(channels, pieces):
    tiles = channels // 128
    ends = [-(-tiles * step // pieces) * 128 for step in range(1, pieces)]
    return list(zip([0] + ends, ends + [channels]))


def back_project(grads, weight):
    return (
        0.5
        * lax.dot_general(
            grads, weight, (((1,), (1,)), ((), ())), preferred_element_type=jnp.float32
        )
    ).astype(jnp.bfloat16)


def per_device(
    student_tokens,
    norm_gain,
    mae_weight,
    clip_target,
    mae_target,
    keep_mask,
    teacher_gate,
    temp_bucket,
):
    samples, frames_here, patches, model_width = student_tokens.shape
    half_rows = patches // 2
    channels = mae_weight.shape[1]
    frame_devices = lax.axis_size("frame")
    top_bit = frame_devices.bit_length() - 2
    weight = lax.all_gather(mae_weight, "fsdp", axis=0, tiled=True)
    token_float = student_tokens.astype(jnp.float32)
    recip = lax.rsqrt(jnp.mean(token_float * token_float, axis=-1, keepdims=True) + epsilon)
    normed = (token_float * recip * norm_gain).astype(jnp.bfloat16)
    keep_float = keep_mask.astype(jnp.float32)
    pooled = (
        jnp.einsum(
            "bfp,bfpd->bfd",
            keep_mask.astype(jnp.bfloat16),
            normed,
            preferred_element_type=jnp.float32,
        )
        / patches
    )
    clip_unit, clip_inverse = unit_rows(pooled)
    teach_unit, _ = unit_rows(clip_target.astype(jnp.float32))
    clip_err = clip_unit - teach_unit
    clip_loss = 0.5 * jnp.sum(clip_err * clip_err, axis=-1)
    scaling = jnp.exp2(temp_bucket.astype(jnp.float32))
    clip_on = (teacher_gate != 2).astype(jnp.float32)
    mae_on = (teacher_gate != 1).astype(jnp.float32)
    parity = lax.axis_index("frame") // (frame_devices // 2)
    halves = normed.reshape(samples, frames_here, 2, half_rows, model_width)
    mask_halves = keep_mask.astype(jnp.bfloat16).reshape(samples, frames_here, 2, half_rows)
    own_half = lax.dynamic_slice_in_dim(halves, parity, 1, 2)[:, :, 0]
    sent_half = lax.dynamic_slice_in_dim(halves, 1 - parity, 1, 2)[:, :, 0]
    own_mask = lax.dynamic_slice_in_dim(mask_halves, parity, 1, 2)[:, :, 0]
    sent_mask = lax.dynamic_slice_in_dim(mask_halves, 1 - parity, 1, 2)[:, :, 0]
    got_half, got_mask = swapped((sent_half, sent_mask), "frame", top_bit)
    mean_rows = (
        (0.5 * (own_half.astype(jnp.float32) + got_half.astype(jnp.float32)))
        .astype(jnp.bfloat16)
        .reshape(-1, model_width)
    )
    live = (own_mask.astype(jnp.float32) * got_mask.astype(jnp.float32)).reshape(samples, -1)
    projected = jnp.dot(mean_rows, weight, preferred_element_type=jnp.float32)
    proj_unit, proj_inverse = unit_rows(projected)
    target_unit, _ = unit_rows(mae_target.reshape(-1, channels).astype(jnp.float32))
    mae_err = proj_unit - target_unit
    mae_loss = (0.5 * jnp.sum(mae_err * mae_err, axis=-1)).reshape(samples, -1)
    sample_loss = scaling * (
        clip_on * jnp.sum(clip_loss, axis=1) + mae_on * jnp.sum(live * mae_loss, axis=1)
    )
    row_scale = ((scaling * mae_on)[:, None] * live).reshape(-1)
    row_grad = (row_scale[:, None] * unit_grad(mae_err, proj_unit, proj_inverse)).astype(
        jnp.bfloat16
    )
    returned = swapped(row_grad, "frame", top_bit)
    clip_count = samples * lax.axis_size("fsdp")
    members = lax.axis_size("fsdp")
    bits = list(range(members.bit_length() - 1))
    orders = [bits, bits[:1] + bits[2:3] + bits[1:2] + bits[3:]]
    parts = []
    for start, stop in channel_cuts(channels, 2):
        part = over_rows(mean_rows, row_grad[:, start:stop])
        parts.append(part.reshape(members, -1, stop - start))
    parts = halving_step(parts, orders, slice(0, 1))
    row_grad, parts = lax.optimization_barrier((row_grad, parts))
    parts = halving_step(parts, orders, slice(1, 2))
    own_grads = row_grad.reshape(samples, frames_here, half_rows, channels)
    got_grads = returned.reshape(samples, frames_here, half_rows, channels)
    lower = jnp.where(parity == 0, own_grads, got_grads)
    upper = jnp.where(parity == 0, got_grads, own_grads)
    both_grads = jnp.stack([lower, upper], axis=2).reshape(-1, channels)
    spread = back_project(both_grads, weight)
    spread, parts = lax.optimization_barrier((spread, parts))
    parts = halving_step(parts, orders, slice(2, 3))
    spread = spread.reshape(samples, frames_here, patches, model_width).astype(jnp.float32)
    clip_grad = (scaling * clip_on)[:, None, None] * unit_grad(clip_err, clip_unit, clip_inverse)
    normed_grad = spread + keep_float[:, :, :, None] * clip_grad[:, :, None, :] / patches
    inner = jnp.mean(normed_grad * norm_gain * token_float, axis=-1, keepdims=True)
    gain_local = jnp.sum(normed_grad * token_float * recip, axis=(0, 1, 2))
    inner, parts = lax.optimization_barrier((inner, parts))
    parts = halving_step(parts, orders, slice(3, None))
    token_grad = (
        recip * (norm_gain * normed_grad - token_float * recip * recip * inner)
    ).astype(jnp.bfloat16)
    token_grad, gain_local = lax.optimization_barrier((token_grad, gain_local))
    loss_local = jnp.sum(sample_loss)
    shards = [part[0] for part in parts]
    sums = jnp.concatenate([gain_local, jnp.full((128,), loss_local)])
    sums = doubled_sum(sums, ("fsdp", "frame"))
    gain_total, loss_total = sums[:model_width], sums[model_width]
    frame_strides = range(frame_devices.bit_length() - 1)
    whole = []
    for shard in shards:
        total = shard.astype(jnp.float32)
        for stride in frame_strides:
            total = lax.reduce_precision(total, 8, 7)
            sent = total.astype(jnp.bfloat16)
            total = total + swapped(sent, "frame", stride).astype(jnp.float32)
        whole.append(total)
    weight_grad = jnp.concatenate(whole, axis=1) / clip_count
    frame_count = frames_here * frame_devices
    gain_grad = gain_total / clip_count
    loss = loss_total / (clip_count * frame_count * patches * channels)
    return (token_grad, weight_grad, gain_grad, loss)


def solution(mesh):
    placed = (
        P("fsdp", "frame", None, None),
        P(),
        P("fsdp", None),
        P("fsdp", "frame", None),
        P("fsdp", "frame", None, None),
        P("fsdp", "frame", None),
        P("fsdp"),
        P("fsdp"),
    )

    return jax.shard_map(
        per_device,
        mesh=mesh,
        in_specs=placed,
        out_specs=(P("fsdp", "frame", None, None), P("fsdp", None), P(), P()),
        check_vma=False,
    )
```
